32 devices in a mesh: seq: 2 (over x), shard: 16 (over z, y, core).
Axes of the slice: x: 2, y: 2, z: 4, core: 2. Of those that a mesh axis runs over, the one named last changes fastest.
Arguments:
- hidden: bfloat16 [2, 32, 1024, 768], P(None, 'shard', 'seq'), may hold values from -6 to 6
- cotangent: bfloat16 [2, 32, 1024, 768], P(None, 'shard', 'seq'), may hold values from -6 to 6
- segments: int32 [2, 32, 1024], P(None, 'shard', 'seq'), may hold values from 0 to 3, never falling along the last dimension, each value on 1 to 512 neighbouring positions
- w_qkv: bfloat16 [768, 2304], P('shard'), may hold values from -0.21875 to 0.21875
- bias_q: bfloat16 [768], P('shard'), may hold values from -3 to 3
- bias_v: bfloat16 [768], P('shard'), may hold values from -0.5 to 0.5
- w_out: bfloat16 [768, 768], P('shard'), may hold values from -1.25 to 1.25
- bias_out: bfloat16 [768], P('shard'), may hold values from -3 to 3
- norm1_gain: bfloat16 [768], P('shard'), may hold values from 0.5 to 1.5
- norm1_bias: bfloat16 [768], P('shard'), may hold values from -3 to 3
- w_up: bfloat16 [768, 3072], P('shard'), may hold values from -0.21875 to 0.21875
- bias_up: bfloat16 [3072], P('shard'), may hold values from -3 to 3
- w_down: bfloat16 [3072, 768], P('shard'), may hold values from -0.109375 to 0.109375
- bias_down: bfloat16 [768], P('shard'), may hold values from -3 to 3
- norm2_gain: bfloat16 [768], P('shard'), may hold values from 0.5 to 1.5
- norm2_bias: bfloat16 [768], P('shard'), may hold values from -3 to 3
Outputs:
- layer_out: bfloat16 [2, 32, 1024, 768], P(None, 'shard', 'seq')
- grad_hidden: bfloat16 [2, 32, 1024, 768], P(None, 'shard', 'seq')
- grad_w_qkv: float32 [768, 2304], P('shard')
- grad_bias_q: float32 [768], P('shard')
- grad_bias_v: float32 [768], P('shard')
- grad_w_out: float32 [768, 768], P('shard')
- grad_bias_out: float32 [768], P('shard')
- grad_norm1_gain: float32 [768], P('shard')
- grad_norm1_bias: float32 [768], P('shard')
- grad_w_up: float32 [768, 3072], P('shard')
- grad_bias_up: float32 [3072], P('shard')
- grad_w_down: float32 [3072, 768], P('shard')
- grad_bias_down: float32 [768], P('shard')
- grad_norm2_gain: float32 [768], P('shard')
- grad_norm2_bias: float32 [768], P('shard')
The draws below stay inside these ranges and needn't reach their ends.
Inputs may be any that keep to these rules, and one draw needn't show every extreme that they name: `segments`: along each sequence of 1024 tokens the document numbers never fall; each of the 4 documents has 1 to 512 tokens, and one has exactly 512.
All inputs are finite; a program needn't handle non-finite values.
Results may differ from the reference program's by a relative error of at most 0.014.
Values may be sent and summed in bfloat16 or wider, within the bound.
No kernel may reach another device: no remote copies, remote signals or barrier semaphores. Data moves between devices by JAX's collectives and lax.ppermute only.
A program may use at most 256 MiB of HBM per device.

```python
import math
import jax
import jax.numpy as jnp
import numpy as np
from jax import lax

D = 768
H = 12
HD = 64
FF = 3072
LEN = 1024
MICRO = 2
BATCH = 32


def strengthened(values, own_key, source, target, blocks, factor):
    def block_of(position):
        return (jnp.arange(values.shape[position]) // (values.shape[position] // blocks)).reshape((-1,) + (1,) * (values.ndim - 1 - position))

    first = jax.random.permutation(own_key, blocks)[block_of(target)]
    far = (block_of(target) + blocks // 2) % blocks
    return jnp.where((block_of(source) == first) | (block_of(source) == far), factor * values, values)


def shard_levels(rng, dims, split, smallest, top_value):
    def one(dim, shards_of):
        steps = jax.random.uniform(jax.random.fold_in(jax.random.fold_in(rng, 6), dim), (shards_of,), jnp.float32, smallest / len(split), top_value / len(split))
        return jnp.repeat(jnp.exp(steps), dims[dim] // shards_of).reshape((-1,) + (1,) * (len(dims) - dim - 1))

    loudness = one(*split[0])
    for cut in split[1:]:
        loudness = loudness * one(*cut)
    return loudness


def split_up(count, total, reach, lean):
    portions = [(1 << 20) // math.isqrt(grade ** lean) + 1 for grade in range(2, count + 1)]
    spare, given = total - reach - (count - 1), [1] * (count - 1)
    while spare > 0:
        candidates = [i for i in range(count - 1) if given[i] < reach]
        pool, budget = sum([portions[i] for i in candidates]), spare
        for i in candidates:
            extra = min(reach - given[i], max(1, budget * portions[i] // pool), spare)
            given[i] = given[i] + extra
            spare = spare - extra
    return np.array([reach] + given)


def uneven_parts(own_key, amount, total, bound, lean):
    if amount == 2:
        one = jax.random.randint(own_key, (), max(1, total - bound), min(bound, total - 1) + 1)
        return jnp.stack([one, total - one])
    sizes = jnp.asarray(split_up(amount, total, bound, lean), jnp.int32)
    couples = (amount - 1) // 2
    giver, taker = sizes[1:1 + 2 * couples:2], sizes[2:2 + 2 * couples:2]
    room = jnp.minimum(giver - 1, bound - taker)
    moved = jax.random.randint(jax.random.fold_in(own_key, 1), (couples,), 0, 1 << 20) % (room + 1)
    sizes = sizes.at[1:1 + 2 * couples:2].set(giver - moved).at[2:2 + 2 * couples:2].set(taker + moved)
    return sizes[jax.random.permutation(jax.random.fold_in(own_key, 2), amount)]


def centred(own_key, shape, deviation, most, pieces=(), held_as=jnp.bfloat16):
    drawn = deviation * jax.random.normal(own_key, shape, jnp.float32)
    if pieces:
        drawn = drawn * shard_levels(own_key, shape, pieces, -0.22, 0.18)
    return jnp.clip(drawn, -most, most).astype(held_as)


def heavy_noise(rng, dims, width, most, pieces, heavy, dtype=jnp.bfloat16):
    entries = width * jax.random.normal(rng, dims, jnp.float32)
    if pieces:
        entries = entries * shard_levels(rng, dims, pieces, -0.22, 0.18)
    return jnp.clip(strengthened(entries, jax.random.fold_in(rng, 3), *heavy), -most, most).astype(dtype)


def setup_inputs(seed: int = 0) -> dict:
    streams_of = jax.random.split(jax.random.key(seed), 17)
    return {
        "hidden": centred(streams_of[0], (MICRO, BATCH, LEN, D), 1.0, 6.0, ((1, 16), (2, 2))),
        "cotangent": heavy_noise(streams_of[1], (MICRO, BATCH, LEN, D), 1.0, 6.0, ((1, 16), (2, 2)), (1, 3, 16, 2.0)),
        "segments": jax.vmap(lambda own: jnp.searchsorted(jnp.cumsum(uneven_parts(own, 4, LEN, LEN // 2, 2)), jnp.arange(LEN), side="right"))(jax.random.split(streams_of[2], MICRO * BATCH)).reshape((MICRO, BATCH, LEN)).astype(jnp.int32),
        "w_qkv": centred(streams_of[3], (D, 3 * D), D ** -0.5, 0.21875, ((0, 16),)),
        "bias_q": centred(streams_of[4], (D,), 0.5, 3.0, ((0, 16),)),
        "bias_v": centred(streams_of[5], (D,), 0.08, 0.5, ((0, 16),)),
        "w_out": centred(streams_of[6], (D, D), (D // 32) ** -0.5, 1.25, ((0, 16),)),
        "bias_out": centred(streams_of[7], (D,), 0.5, 3.0, ((0, 16),)),
        "norm1_gain": jnp.clip(1.0 + 0.1 * jax.random.normal(streams_of[8], (D,), jnp.float32), 0.5, 1.5).astype(jnp.bfloat16),
        "norm1_bias": centred(streams_of[9], (D,), 0.5, 3.0, ((0, 16),)),
        "w_up": centred(streams_of[10], (D, FF), D ** -0.5, 0.21875, ((0, 16),)),
        "bias_up": centred(streams_of[11], (FF,), 0.5, 3.0, ((0, 16),)),
        "w_down": centred(streams_of[12], (FF, D), FF ** -0.5, 0.109375, ((0, 16),)),
        "bias_down": centred(streams_of[13], (D,), 0.5, 3.0, ((0, 16),)),
        "norm2_gain": jnp.clip(1.0 + 0.1 * jax.random.normal(streams_of[14], (D,), jnp.float32), 0.5, 1.5).astype(jnp.bfloat16),
        "norm2_bias": centred(streams_of[15], (D,), 0.5, 3.0, ((0, 16),)),
    }


@jax.custom_vjp
def low(v):
    return lax.optimization_barrier(v.astype(jnp.bfloat16)).astype(jnp.float32)

@jax.custom_vjp
def low_back(v):
    return v

def low_keep(v):
    return (low(v), None)

def low_pass(kept, grad):
    return (grad,)

def back_keep(v):
    return (v, None)

def back_low(kept, grad):
    return (low(grad),)
low.defvjp(low_keep, low_pass)
low_back.defvjp(back_keep, back_low)
highest = lax.Precision.HIGHEST
eps_norm = 1e-05
masked_score = -1e+30

def norm_apply(resid, gain, offset):
    center = lax.optimization_barrier(jnp.mean(resid, axis=-1, keepdims=True))
    deviate = resid - center
    spread = lax.optimization_barrier(jnp.mean(deviate * deviate, axis=-1, keepdims=True))
    return deviate * lax.rsqrt(spread + eps_norm) * gain + offset

def layer(inputs, doc_row, params):
    proj_weight, query_bias, value_bias, attn_weight, attn_bias, gain_first, shift_first, upper_weight, upper_bias, lower_weight, lower_bias, gain_second, shift_second = params
    seq_length = inputs.shape[0]
    model_width = inputs.shape[1]
    score_scale = HD ** (-0.5)
    offsets = jnp.concatenate([query_bias, jnp.zeros_like(query_bias), value_bias])
    projected = low_back(low(jnp.dot(inputs, proj_weight, precision=highest) + offsets))

    def to_heads(columns_part):
        return columns_part.reshape(seq_length, H, HD).transpose(1, 0, 2)
    queries = to_heads(projected[:, :model_width])
    keys_heads = to_heads(projected[:, model_width:2 * model_width])
    values_heads = to_heads(projected[:, 2 * model_width:])
    same_doc = doc_row[:, None] == doc_row[None, :]

    def one_head(element):
        query_head, key_head, value_head = element
        scores = low_back(jnp.dot(query_head, key_head.T, precision=highest) * score_scale)
        scores = jnp.where(same_doc, scores, masked_score)
        raised = jnp.exp(scores - lax.optimization_barrier(jnp.max(scores, axis=1, keepdims=True)))
        soft_probs = raised / lax.optimization_barrier(jnp.sum(raised, axis=1, keepdims=True))
        return jnp.dot(low(soft_probs), value_head, precision=highest)
    context = lax.map(jax.checkpoint(one_head), (queries, keys_heads, values_heads))
    context = low_back(low(context.transpose(1, 0, 2).reshape(seq_length, model_width)))
    attn_out = low_back(jnp.dot(context, attn_weight, precision=highest) + attn_bias)
    normed_first = norm_apply(inputs + attn_out, gain_first, shift_first)
    upper_pre = low_back(jnp.dot(low(normed_first), upper_weight, precision=highest) + upper_bias)
    activated = low(jax.nn.gelu(upper_pre, approximate=False))
    lower_out = low_back(jnp.dot(activated, lower_weight, precision=highest) + lower_bias)
    return norm_apply(normed_first + lower_out, gain_second, shift_second)

def reference(hidden, cotangent, segments, w_qkv, bias_q, bias_v, w_out, bias_out, norm1_gain, norm1_bias, w_up, bias_up, w_down, bias_down, norm2_gain, norm2_bias):
    params = tuple((argument.astype(jnp.float32) for argument in (w_qkv, bias_q, bias_v, w_out, bias_out, norm1_gain, norm1_bias, w_up, bias_up, w_down, bias_down, norm2_gain, norm2_bias)))
    inputs_all = hidden.astype(jnp.float32).reshape(-1, LEN, D)
    upstream_all = cotangent.astype(jnp.float32).reshape(-1, LEN, D)
    doc_all = segments.reshape(-1, LEN)

    def one_sequence(accum, element):
        inputs, upstream, doc_row = element

        def forward(values, *weights):
            return layer(values, doc_row, weights)
        result, pullback = jax.vjp(forward, inputs, *params)
        gradients = pullback(upstream)
        accum = tuple((left + right for left, right in zip(accum, gradients[1:])))
        return (accum, (result.astype(jnp.bfloat16), gradients[0].astype(jnp.bfloat16)))
    zero_grads = tuple((jnp.zeros(argument.shape, jnp.float32) for argument in params))
    totals, (results, grads_in) = lax.scan(one_sequence, zero_grads, (inputs_all, upstream_all, doc_all))
    return (results.reshape(hidden.shape), grads_in.reshape(hidden.shape), totals[0], totals[1], totals[2], totals[3], totals[4], totals[5], totals[6], totals[7], totals[8], totals[9], totals[10], totals[11], totals[12])
```

```python
import jax
import jax.numpy as jnp
from jax import lax
from jax.experimental import pallas as pl
from jax.experimental.pallas import tpu as pltpu
from jax.sharding import PartitionSpec as P

HD = 64
PAIR = 2 * HD
QB = 256
UNIT = 128
eps_norm = 1e-05
masked_score = -1e30
bf16 = jnp.bfloat16
f32 = jnp.float32
NT = (((1,), (1,)), ((), ()))
TN = (((0,), (0,)), ((), ()))


def dot(a, b, dims=(((1,), (0,)), ((), ()))):
    return lax.dot_general(a, b, dims, preferred_element_type=f32)


def window_sizes(seq_length):
    units = seq_length // UNIT
    sizes = [n for n in (2, 3, 4, 5, 6) if n < units]
    return sizes + [units]


def key_windows(doc):
    count, seq_length = doc.shape
    first_doc = doc[:, ::QB]
    last_doc = doc[:, QB - 1 :: QB]
    low = jnp.sum((doc[:, None, :] < first_doc[:, :, None]).astype(jnp.int32), axis=2)
    high = jnp.sum((doc[:, None, :] <= last_doc[:, :, None]).astype(jnp.int32), axis=2)
    low_unit = low // UNIT
    need = (high + UNIT - 1) // UNIT - low_unit
    sizes = window_sizes(seq_length)
    size = jnp.full_like(need, sizes[-1])
    for n in sizes[::-1]:
        size = jnp.where(need <= n, n, size)
    start = jnp.minimum(low_unit, seq_length // UNIT - size)
    return start, size


def head_masks():
    lane = lax.broadcasted_iota(jnp.int32, (1, PAIR), 1)
    first = (lane < HD).astype(f32)
    return first.astype(bf16), (1.0 - first).astype(bf16)


def fwd_body(start_ref, size_ref, q_ref, k_ref, v_ref, dcol_ref, drow_ref, o_ref, lse_ref):
    item = pl.program_id(0)
    seq_length = q_ref.shape[0]
    masks = head_masks()
    first_lane = lax.broadcasted_iota(jnp.int32, (QB, PAIR), 1) < HD

    def step(i, carry):
        rows = pl.ds(pl.multiple_of(i * QB, QB), QB)
        for n in window_sizes(seq_length):

            @pl.when(size_ref[item, i] == n)
            def _():
                keys = pl.ds(pl.multiple_of(start_ref[item, i] * UNIT, UNIT), n * UNIT)
                q = q_ref[rows, :] * jnp.asarray(HD**-0.5, bf16)
                k = k_ref[keys, :]
                v = v_ref[keys, :]
                same = dcol_ref[rows, :] == drow_ref[:, keys]
                outs = []
                lses = []
                for h in range(2):
                    s = jnp.where(same, dot(q * masks[h], k, NT), masked_score)
                    top = jnp.max(s, axis=1, keepdims=True)
                    p = jnp.exp(s - top)
                    total = jnp.sum(p, axis=1, keepdims=True)
                    outs.append(dot(p.astype(bf16), v) * (1.0 / total))
                    lses.append(top + jnp.log(total))
                o_ref[rows, :] = jnp.where(first_lane, outs[0], outs[1]).astype(bf16)
                lse = jnp.where(first_lane, lses[0], lses[1]).T
                lse_ref[0:1, rows] = lse[0:1, :]
                lse_ref[1:2, rows] = lse[HD : HD + 1, :]

        return carry

    lax.fori_loop(0, seq_length // QB, step, 0)


def attend_forward(proj, start, size, doc_col, doc_row):
    count, seq_length, columns = proj.shape
    width = columns // 3
    pairs = width // PAIR

    def part(offset):
        return pl.BlockSpec((None, seq_length, PAIR), lambda s, p, *_: (s, 0, p + offset * pairs))

    return pl.pallas_call(
        fwd_body,
        grid_spec=pltpu.PrefetchScalarGridSpec(
            num_scalar_prefetch=2,
            grid=(count, pairs),
            in_specs=[
                part(0),
                part(1),
                part(2),
                pl.BlockSpec((None, seq_length, 1), lambda s, p, *_: (s, 0, 0)),
                pl.BlockSpec((None, 1, seq_length), lambda s, p, *_: (s, 0, 0)),
            ],
            out_specs=[
                part(0),
                pl.BlockSpec((None, None, 2, seq_length), lambda s, p, *_: (s, p, 0, 0)),
            ],
        ),
        out_shape=[
            jax.ShapeDtypeStruct((count, seq_length, width), bf16),
            jax.ShapeDtypeStruct((count, pairs, 2, seq_length), f32),
        ],
        name="attend_forward",
    )(start, size, proj, proj, proj, doc_col, doc_row)


def bwd_body(
    start_ref, size_ref, q_ref, k_ref, v_ref, dcol_ref, drow_ref, o_ref, do_ref, lse_ref,
    dq_ref, dk_ref, dv_ref, dk_acc, dv_acc,
):
    item = pl.program_id(0)
    seq_length = q_ref.shape[0]
    masks = head_masks()
    first_lane = lax.broadcasted_iota(jnp.int32, (QB, PAIR), 1) < HD
    dk_acc[...] = jnp.zeros_like(dk_acc)
    dv_acc[...] = jnp.zeros_like(dv_acc)

    def step(i, carry):
        rows = pl.ds(pl.multiple_of(i * QB, QB), QB)
        for n in window_sizes(seq_length):

            @pl.when(size_ref[item, i] == n)
            def _():
                keys = pl.ds(pl.multiple_of(start_ref[item, i] * UNIT, UNIT), n * UNIT)
                q = q_ref[rows, :] * jnp.asarray(HD**-0.5, bf16)
                k = k_ref[keys, :]
                v = v_ref[keys, :]
                do = do_ref[rows, :]
                same = dcol_ref[keys, :] == drow_ref[:, rows]
                products = (do.astype(f32) * o_ref[rows, :].astype(f32)).T
                dqs = []
                dk = dv = None
                for h in range(2):
                    qh = q * masks[h]
                    doh = do * masks[h]
                    inner = jnp.sum(products[h * HD : (h + 1) * HD, :], axis=0, keepdims=True)
                    s = dot(k, qh, NT) - lse_ref[h : h + 1, rows]
                    p = jnp.exp(jnp.where(same, s, masked_score))
                    ds = (p * (dot(v, doh, NT) - inner)).astype(bf16)
                    dv_part = dot(p.astype(bf16), doh)
                    dk_part = dot(ds, qh)
                    dv = dv_part if dv is None else dv + dv_part
                    dk = dk_part if dk is None else dk + dk_part
                    dqs.append(dot(ds, k, TN))
                dk_acc[keys, :] += dk
                dv_acc[keys, :] += dv
                dq = jnp.where(first_lane, dqs[0], dqs[1]) * (HD**-0.5)
                dq_ref[rows, :] = dq.astype(bf16)

        return carry

    lax.fori_loop(0, seq_length // QB, step, 0)
    dk_ref[...] = dk_acc[...].astype(bf16)
    dv_ref[...] = dv_acc[...].astype(bf16)


def attend_backward(proj, start, size, doc_col, doc_row, context, d_context, lse):
    count, seq_length, columns = proj.shape
    width = columns // 3
    pairs = width // PAIR

    def part(offset):
        return pl.BlockSpec((None, seq_length, PAIR), lambda s, p, *_: (s, 0, p + offset * pairs))

    grad = jax.ShapeDtypeStruct((count, seq_length, width), bf16)
    return pl.pallas_call(
        bwd_body,
        grid_spec=pltpu.PrefetchScalarGridSpec(
            num_scalar_prefetch=2,
            grid=(count, pairs),
            in_specs=[
                part(0),
                part(1),
                part(2),
                pl.BlockSpec((None, seq_length, 1), lambda s, p, *_: (s, 0, 0)),
                pl.BlockSpec((None, 1, seq_length), lambda s, p, *_: (s, 0, 0)),
                part(0),
                part(0),
                pl.BlockSpec((None, None, 2, seq_length), lambda s, p, *_: (s, p, 0, 0)),
            ],
            out_specs=[part(0), part(0), part(0)],
            scratch_shapes=[
                pltpu.VMEM((seq_length, PAIR), f32),
                pltpu.VMEM((seq_length, PAIR), f32),
            ],
        ),
        out_shape=[grad, grad, grad],
        name="attend_backward",
    )(start, size, proj, proj, proj, doc_col, doc_row, context, d_context, lse)


def norm_parts(resid):
    center = jnp.mean(resid, axis=1, keepdims=True)
    deviate = resid - center
    spread = jnp.mean(deviate * deviate, axis=1, keepdims=True)
    rstd = lax.rsqrt(spread + eps_norm)
    return deviate * rstd, rstd


def norm_back(grad, xhat, rstd):
    return rstd * (
        grad
        - jnp.mean(grad, axis=1, keepdims=True)
        - xhat * jnp.mean(grad * xhat, axis=1, keepdims=True)
    )


def middle_body(
    x_ref, o_ref, g_ref, w_out_ref, w_up_ref, w_down_ref, vec_ref, bias_up_ref,
    out_ref, d_attn_ref, d_context_ref, h1_ref, act_ref, d_up_ref, d_down_ref,
    sums_ref, sums_up_ref, slope_ref,
):
    @pl.when(pl.program_id(0) == 0)
    def _():
        sums_ref[...] = jnp.zeros_like(sums_ref)
        sums_up_ref[...] = jnp.zeros_like(sums_up_ref)

    hidden_units = w_up_ref.shape[1]
    chunk = w_up_ref.shape[0]
    chunks = [slice(c, c + chunk) for c in range(0, hidden_units, chunk)]
    bias_out, gain1, shift1, bias_down, gain2, shift2 = (vec_ref[r : r + 1, :] for r in range(6))
    xhat1, rstd1 = norm_parts(x_ref[...].astype(f32) + dot(o_ref[...], w_out_ref[...]) + bias_out)
    h1 = xhat1 * gain1 + shift1
    h1_low = h1.astype(bf16)
    h1_ref[...] = h1_low
    resid2 = h1 + bias_down
    for c in chunks:
        up = dot(h1_low, w_up_ref[:, c]) + bias_up_ref[:, c]
        cdf = 0.5 + 0.5 * lax.erf(up * (0.5**0.5))
        act = (up * cdf).astype(bf16)
        slope_ref[:, c] = cdf + up * jnp.exp(-0.5 * up * up) * 0.3989422804014327
        act_ref[:, c] = act
        resid2 = resid2 + dot(act, w_down_ref[c, :])
    xhat2, rstd2 = norm_parts(resid2)
    out_ref[...] = (xhat2 * gain2 + shift2).astype(bf16)
    g = g_ref[...].astype(f32)
    d_resid2 = norm_back(g * gain2, xhat2, rstd2)
    d_down = d_resid2.astype(bf16)
    d_down_ref[...] = d_down
    d_h1 = d_resid2
    for c in chunks:
        d_up = (dot(d_down, w_down_ref[c, :], NT) * slope_ref[:, c]).astype(bf16)
        d_up_ref[:, c] = d_up
        sums_up_ref[:, c] += jnp.sum(d_up.astype(f32), axis=0, keepdims=True)
        d_h1 = d_h1 + dot(d_up, w_up_ref[:, c], NT)
    d_attn = norm_back(d_h1 * gain1, xhat1, rstd1).astype(bf16)
    d_attn_ref[...] = d_attn
    d_context_ref[...] = dot(d_attn, w_out_ref[...], NT).astype(bf16)
    rows = (d_attn.astype(f32), d_h1 * xhat1, d_h1, d_down.astype(f32), g * xhat2, g)
    for r, value in enumerate(rows):
        sums_ref[r : r + 1, :] += jnp.sum(value, axis=0, keepdims=True)


def middle(x, context, g, w_out, w_up, w_down, vectors, bias_up):
    tokens, width = x.shape
    hidden_units = w_up.shape[1]
    tile = QB

    def rows(columns):
        return pl.BlockSpec((tile, columns), lambda i: (i, 0))

    def whole(shape, mode=None):
        return pl.BlockSpec(shape, lambda i: (0, 0), pipeline_mode=mode)

    once = pl.Buffered(1)
    narrow = jax.ShapeDtypeStruct((tokens, width), bf16)
    wide = jax.ShapeDtypeStruct((tokens, hidden_units), bf16)
    return pl.pallas_call(
        middle_body,
        grid=(tokens // tile,),
        in_specs=[
            rows(width),
            rows(width),
            rows(width),
            whole(w_out.shape, once),
            whole(w_up.shape, once),
            whole(w_down.shape, once),
            whole(vectors.shape, once),
            whole(bias_up.shape, once),
        ],
        out_specs=[
            rows(width),
            rows(width),
            rows(width),
            rows(width),
            rows(hidden_units),
            rows(hidden_units),
            rows(width),
            whole((8, width)),
            whole((1, hidden_units)),
        ],
        out_shape=[
            narrow,
            narrow,
            narrow,
            narrow,
            wide,
            wide,
            narrow,
            jax.ShapeDtypeStruct((8, width), f32),
            jax.ShapeDtypeStruct((1, hidden_units), f32),
        ],
        scratch_shapes=[pltpu.VMEM((tile, hidden_units), f32)],
        name="middle",
    )(x, context, g, w_out, w_up, w_down, vectors, bias_up)


def gather_rows(part):
    return lax.all_gather(part, "shard", axis=0, tiled=True)


def own_sum(part):
    return lax.psum(lax.psum_scatter(part, "shard", scatter_dimension=0, tiled=True), "seq")


def own_sum_low(part):
    piece = lax.psum_scatter(part.astype(bf16), "shard", scatter_dimension=0, tiled=True)
    return jnp.sum(lax.all_gather(piece, "seq").astype(f32), axis=0)


def local(
    hidden, cotangent, segments, w_qkv, bias_q, bias_v, w_out, bias_out, norm1_gain, norm1_bias,
    w_up, bias_up, w_down, bias_down, norm2_gain, norm2_bias,
):
    micro, batch, part_length, width = hidden.shape

    def to_whole(rows):
        merged = rows.reshape((micro * batch,) + rows.shape[2:])
        return lax.all_to_all(merged, "seq", split_axis=0, concat_axis=1, tiled=True)

    def to_parts(rows):
        back = lax.all_to_all(rows, "seq", split_axis=1, concat_axis=0, tiled=True)
        return back.reshape(hidden.shape)

    x = to_whole(hidden)
    doc = to_whole(segments)
    count, seq_length = doc.shape
    tokens = count * seq_length
    start, size = key_windows(doc)
    doc_col = doc[:, :, None]
    doc_row = doc[:, None, :]
    full_qkv = gather_rows(w_qkv)
    narrow = jnp.stack(
        [bias_q, bias_v, bias_out, norm1_gain, norm1_bias, bias_down, norm2_gain, norm2_bias]
    )
    small = jnp.concatenate([narrow.reshape(-1), bias_up])[None, :]
    small = gather_rows(small).astype(f32)
    split = narrow.size
    vectors = small[:, :split].reshape(-1, 8, narrow.shape[1]).transpose(1, 0, 2).reshape(8, width)
    full_bias_up = small[:, split:].reshape(1, -1)
    full_out = gather_rows(w_out)
    full_up = gather_rows(w_up)
    full_down = gather_rows(w_down)
    g = to_whole(cotangent)

    x_rows = x.reshape(tokens, width)
    offsets = jnp.concatenate([vectors[0], jnp.zeros_like(vectors[0]), vectors[1]])
    proj = (dot(x_rows, full_qkv) + offsets).astype(bf16).reshape(count, seq_length, -1)
    context, lse = attend_forward(proj, start, size, doc_col, doc_row)
    context_rows = context.reshape(tokens, width)
    out, d_attn, d_context, h1, act, d_up, d_down, sums, sums_up = middle(
        x_rows,
        context_rows,
        g.reshape(tokens, width),
        full_out,
        full_up,
        full_down,
        vectors[2:],
        full_bias_up,
    )
    layer_out = to_parts(out.reshape(count, seq_length, width))
    grad_down = own_sum_low(dot(act, d_down, TN))
    grad_up = own_sum_low(dot(h1, d_up, TN))
    grad_out = own_sum_low(dot(context_rows, d_attn, TN))
    dq, dk, dv = attend_backward(
        proj,
        start,
        size,
        doc_col,
        doc_row,
        context,
        d_context.reshape(count, seq_length, width),
        lse,
    )
    d_proj = [d.reshape(tokens, width) for d in (dq, dk, dv)]
    grad_qkv = own_sum_low(jnp.concatenate([dot(x_rows, d, TN) for d in d_proj], axis=1))
    grad_x = d_attn.astype(f32)
    for index, d in enumerate(d_proj):
        grad_x = grad_x + dot(d, full_qkv[:, index * width : (index + 1) * width], NT)
    grad_hidden = to_parts(grad_x.astype(bf16).reshape(count, seq_length, width))
    sum_q, sum_v = (jnp.sum(d_proj[i].astype(f32), axis=0) for i in (0, 2))
    shards = width // narrow.shape[1]
    stacked = jnp.concatenate([sum_q[None], sum_v[None], sums[:6]], axis=0)
    stacked = stacked.reshape(8, shards, -1).transpose(1, 0, 2).reshape(shards, -1)
    stacked = jnp.concatenate([stacked, sums_up.reshape(shards, -1)], axis=1)
    totals = own_sum(stacked)[0]
    owned = totals[:split].reshape(8, -1)
    return (
        layer_out,
        grad_hidden,
        grad_qkv,
        owned[0],
        owned[1],
        grad_out,
        owned[2],
        owned[3],
        owned[4],
        grad_up,
        totals[split:],
        grad_down,
        owned[5],
        owned[6],
        owned[7],
    )


def solution(mesh):
    tokens = P(None, "shard", "seq", None)
    matrix = P("shard", None)
    vector = P("shard")
    params = (
        matrix, vector, vector, matrix, vector, vector, vector, matrix, vector, matrix, vector,
        vector, vector,
    )
    return jax.shard_map(
        local,
        mesh=mesh,
        in_specs=(tokens, tokens, P(None, "shard", "seq")) + params,
        out_specs=(tokens, tokens) + params,
        check_vma=False,
    )
```

```python
import functools

import jax
import jax.numpy as jnp
from jax import lax
from jax.experimental import pallas as pl
from jax.experimental.pallas import tpu as pltpu
from jax.sharding import PartitionSpec as P


HD = 64
PAIR = 2 * HD
QB = 256
UNIT = 128
GROUPS = 1
eps_norm = 1e-05
masked_score = -1e30
bf16 = jnp.bfloat16
f32 = jnp.float32
NT = (((1,), (1,)), ((), ()))
TN = (((0,), (0,)), ((), ()))


def dot(a, b, dims=(((1,), (0,)), ((), ()))):
    return lax.dot_general(a, b, dims, preferred_element_type=f32)


def window_sizes(seq_length):
    units = seq_length // UNIT
    sizes = [n for n in (2, 3, 4, 5, 6) if n < units]
    return sizes + [units]


def key_windows(doc):
    _, seq_length = doc.shape
    first_doc = doc[:, ::QB]
    last_doc = doc[:, QB - 1 :: QB]
    low = jnp.sum((doc[:, None, :] < first_doc[:, :, None]).astype(jnp.int32), axis=2)
    high = jnp.sum((doc[:, None, :] <= last_doc[:, :, None]).astype(jnp.int32), axis=2)
    low_unit = low // UNIT
    need = (high + UNIT - 1) // UNIT - low_unit
    sizes = window_sizes(seq_length)
    size = jnp.full_like(need, sizes[-1])
    for n in sizes[::-1]:
        size = jnp.where(need <= n, n, size)
    start = jnp.minimum(low_unit, seq_length // UNIT - size)
    return start, size


def head_masks():
    lane = lax.broadcasted_iota(jnp.int32, (1, PAIR), 1)
    first = (lane < HD).astype(f32)
    return first.astype(bf16), (1.0 - first).astype(bf16)


def fwd_body(start_ref, size_ref, q_ref, k_ref, v_ref, dcol_ref, drow_ref, o_ref, lse_ref):
    item = pl.program_id(0)
    seq_length = q_ref.shape[0]
    masks = head_masks()
    first_lane = lax.broadcasted_iota(jnp.int32, (QB, PAIR), 1) < HD

    def step(i, carry):
        rows = pl.ds(pl.multiple_of(i * QB, QB), QB)
        for n in window_sizes(seq_length):

            @pl.when(size_ref[item, i] == n)
            def _():
                keys = pl.ds(pl.multiple_of(start_ref[item, i] * UNIT, UNIT), n * UNIT)
                q = q_ref[rows, :] * jnp.asarray(HD**-0.5, bf16)
                k = k_ref[keys, :]
                v = v_ref[keys, :]
                same = dcol_ref[rows, :] == drow_ref[:, keys]
                outs = []
                lses = []
                for h in range(2):
                    s = jnp.where(same, dot(q * masks[h], k, NT), masked_score)
                    top = jnp.max(s, axis=1, keepdims=True)
                    p = jnp.exp(s - top)
                    total = jnp.sum(p, axis=1, keepdims=True)
                    outs.append(dot(p.astype(bf16), v) * (1.0 / total))
                    lses.append(top + jnp.log(total))
                o_ref[rows, :] = jnp.where(first_lane, outs[0], outs[1]).astype(bf16)
                lse = jnp.where(first_lane, lses[0], lses[1]).T
                lse_ref[0:1, rows] = lse[0:1, :]
                lse_ref[1:2, rows] = lse[HD : HD + 1, :]

        return carry

    lax.fori_loop(0, seq_length // QB, step, 0)


def column_block(seq_length, base):
    return pl.BlockSpec((None, seq_length, PAIR), lambda s, p, *_: (s, 0, p + base))


def attend_forward(proj, start, size, doc_col, doc_row, group):
    count, seq_length, columns = proj.shape
    all_pairs = columns // 3 // PAIR
    pairs = all_pairs // GROUPS

    def part(index):
        return column_block(seq_length, index * all_pairs + group * pairs)

    return pl.pallas_call(
        fwd_body,
        grid_spec=pltpu.PrefetchScalarGridSpec(
            num_scalar_prefetch=2,
            grid=(count, pairs),
            in_specs=[
                part(0),
                part(1),
                part(2),
                pl.BlockSpec((None, seq_length, 1), lambda s, p, *_: (s, 0, 0)),
                pl.BlockSpec((None, 1, seq_length), lambda s, p, *_: (s, 0, 0)),
            ],
            out_specs=[
                column_block(seq_length, 0),
                pl.BlockSpec((None, None, 2, seq_length), lambda s, p, *_: (s, p, 0, 0)),
            ],
        ),
        out_shape=[
            jax.ShapeDtypeStruct((count, seq_length, pairs * PAIR), bf16),
            jax.ShapeDtypeStruct((count, pairs, 2, seq_length), f32),
        ],
        cost_estimate=pl.CostEstimate(
            flops=16 * count * pairs * seq_length**2 * PAIR, transcendentals=0, bytes_accessed=0
        ),
        name="attend_forward",
    )(start, size, proj, proj, proj, doc_col, doc_row)


def bwd_body(
    start_ref, size_ref, q_ref, k_ref, v_ref, dcol_ref, drow_ref, o_ref, do_ref, lse_ref,
    grad_ref, sums_ref, dk_acc, dv_acc,
):
    item = pl.program_id(0)
    seq_length = q_ref.shape[0]
    masks = head_masks()
    first_lane = lax.broadcasted_iota(jnp.int32, (QB, PAIR), 1) < HD
    dk_acc[...] = jnp.zeros_like(dk_acc)
    dv_acc[...] = jnp.zeros_like(dv_acc)
    sums_ref[...] = jnp.zeros_like(sums_ref)

    def step(i, carry):
        rows = pl.ds(pl.multiple_of(i * QB, QB), QB)
        for n in window_sizes(seq_length):

            @pl.when(size_ref[item, i] == n)
            def _():
                keys = pl.ds(pl.multiple_of(start_ref[item, i] * UNIT, UNIT), n * UNIT)
                q = q_ref[rows, :] * jnp.asarray(HD**-0.5, bf16)
                k = k_ref[keys, :]
                v = v_ref[keys, :]
                do = do_ref[rows, :]
                same = dcol_ref[keys, :] == drow_ref[:, rows]
                products = (do.astype(f32) * o_ref[rows, :].astype(f32)).T
                dqs = []
                dk = dv = None
                for h in range(2):
                    qh = q * masks[h]
                    doh = do * masks[h]
                    inner = jnp.sum(products[h * HD : (h + 1) * HD, :], axis=0, keepdims=True)
                    s = dot(k, qh, NT) - lse_ref[h : h + 1, rows]
                    p = jnp.exp(jnp.where(same, s, masked_score))
                    ds = (p * (dot(v, doh, NT) - inner)).astype(bf16)
                    dv_part = dot(p.astype(bf16), doh)
                    dk_part = dot(ds, qh)
                    dv = dv_part if dv is None else dv + dv_part
                    dk = dk_part if dk is None else dk + dk_part
                    dqs.append(dot(ds, k, TN))
                dk_acc[keys, :] += dk
                dv_acc[keys, :] += dv
                dq = (jnp.where(first_lane, dqs[0], dqs[1]) * (HD**-0.5)).astype(bf16)
                grad_ref[0, rows, :] = dq
                sums_ref[0:1, :] += jnp.sum(dq.astype(f32), axis=0, keepdims=True)

        return carry

    lax.fori_loop(0, seq_length // QB, step, 0)
    grad_ref[1] = dk_acc[...].astype(bf16)
    dv = dv_acc[...].astype(bf16)
    grad_ref[2] = dv
    sums_ref[1:2, :] = jnp.sum(dv.astype(f32), axis=0, keepdims=True)


def attend_backward(proj, start, size, doc_col, doc_row, context, d_context, lse, group):
    count, seq_length, columns = proj.shape
    all_pairs = columns // 3 // PAIR
    pairs = all_pairs // GROUPS

    def part(index):
        return column_block(seq_length, index * all_pairs + group * pairs)

    return pl.pallas_call(
        bwd_body,
        grid_spec=pltpu.PrefetchScalarGridSpec(
            num_scalar_prefetch=2,
            grid=(count, pairs),
            in_specs=[
                part(0),
                part(1),
                part(2),
                pl.BlockSpec((None, seq_length, 1), lambda s, p, *_: (s, 0, 0)),
                pl.BlockSpec((None, 1, seq_length), lambda s, p, *_: (s, 0, 0)),
                column_block(seq_length, 0),
                column_block(seq_length, 0),
                pl.BlockSpec((None, None, 2, seq_length), lambda s, p, *_: (s, p, 0, 0)),
            ],
            out_specs=[
                pl.BlockSpec((3, None, seq_length, PAIR), lambda s, p, *_: (0, s, 0, p)),
                pl.BlockSpec((None, 2, PAIR), lambda s, p, *_: (s, 0, p)),
            ],
            scratch_shapes=[
                pltpu.VMEM((seq_length, PAIR), f32),
                pltpu.VMEM((seq_length, PAIR), f32),
            ],
        ),
        out_shape=[
            jax.ShapeDtypeStruct((3, count, seq_length, pairs * PAIR), bf16),
            jax.ShapeDtypeStruct((count, 2, pairs * PAIR), f32),
        ],
        cost_estimate=pl.CostEstimate(
            flops=24 * count * pairs * seq_length**2 * PAIR, transcendentals=0, bytes_accessed=0
        ),
        name="attend_backward",
    )(start, size, proj, proj, proj, doc_col, doc_row, context, d_context, lse)


def norm_parts(resid):
    center = jnp.mean(resid, axis=1, keepdims=True)
    deviate = resid - center
    spread = jnp.mean(deviate * deviate, axis=1, keepdims=True)
    rstd = lax.rsqrt(spread + eps_norm)
    return deviate * rstd, rstd


def norm_back(grad, xhat, rstd):
    return rstd * (
        grad
        - jnp.mean(grad, axis=1, keepdims=True)
        - xhat * jnp.mean(grad * xhat, axis=1, keepdims=True)
    )


def middle_body(
    x_ref, g_ref, w_out_ref, vec_ref, bias_up_ref, *refs
):
    chunk = x_ref.shape[1]
    chunks = [slice(c, c + chunk) for c in range(0, bias_up_ref.shape[1], chunk)]
    w_up_refs, refs = refs[: len(chunks)], refs[len(chunks) :]
    w_down_refs, refs = refs[: len(chunks)], refs[len(chunks) :]
    o_refs, refs = refs[:GROUPS], refs[GROUPS:]
    d_context_refs, refs = refs[:GROUPS], refs[GROUPS:]
    out_ref, d_attn_ref, h1_ref, act_ref, d_up_ref, d_down_ref, sums_ref, sums_up_ref, slope_ref = refs
    span = o_refs[0].shape[1]

    @pl.when(pl.program_id(0) == 0)
    def _():
        sums_ref[...] = jnp.zeros_like(sums_ref)
        sums_up_ref[...] = jnp.zeros_like(sums_up_ref)

    bias_out, gain1, shift1, bias_down, gain2, shift2 = (vec_ref[r : r + 1, :] for r in range(6))
    resid1 = x_ref[...].astype(f32) + bias_out
    for j, o_ref in enumerate(o_refs):
        resid1 = resid1 + dot(o_ref[...], w_out_ref[j * span : (j + 1) * span, :])
    xhat1, rstd1 = norm_parts(resid1)
    h1 = xhat1 * gain1 + shift1
    h1_low = h1.astype(bf16)
    h1_ref[...] = h1_low
    resid2 = h1 + bias_down
    for c, w_up_ref, w_down_ref in zip(chunks, w_up_refs, w_down_refs):
        up = dot(h1_low, w_up_ref[...]) + bias_up_ref[:, c]
        cdf = 0.5 + 0.5 * lax.erf(up * (0.5**0.5))
        act = (up * cdf).astype(bf16)
        slope_ref[:, c] = cdf + up * jnp.exp(-0.5 * up * up) * 0.3989422804014327
        act_ref[:, c] = act
        resid2 = resid2 + dot(act, w_down_ref[...])
    xhat2, rstd2 = norm_parts(resid2)
    out_ref[...] = (xhat2 * gain2 + shift2).astype(bf16)
    g = g_ref[...].astype(f32)
    d_resid2 = norm_back(g * gain2, xhat2, rstd2)
    d_down = d_resid2.astype(bf16)
    d_down_ref[...] = d_down
    d_h1 = d_resid2
    for c, w_up_ref, w_down_ref in zip(chunks, w_up_refs, w_down_refs):
        d_up = (dot(d_down, w_down_ref[...], NT) * slope_ref[:, c]).astype(bf16)
        d_up_ref[:, c] = d_up
        sums_up_ref[:, c] += jnp.sum(d_up.astype(f32), axis=0, keepdims=True)
        d_h1 = d_h1 + dot(d_up, w_up_ref[...], NT)
    d_attn = norm_back(d_h1 * gain1, xhat1, rstd1).astype(bf16)
    d_attn_ref[...] = d_attn
    for j, ref in enumerate(d_context_refs):
        ref[...] = dot(d_attn, w_out_ref[j * span : (j + 1) * span, :], NT).astype(bf16)
    rows = (d_attn.astype(f32), d_h1 * xhat1, d_h1, d_down.astype(f32), g * xhat2, g)
    for r, value in enumerate(rows):
        sums_ref[r : r + 1, :] += jnp.sum(value, axis=0, keepdims=True)


def middle(x, contexts, g, w_packed, vectors, bias_up):
    tokens, width = x.shape
    hidden_units = bias_up.shape[1]
    blocks = hidden_units // width
    tile = QB

    def rows(columns):
        return pl.BlockSpec((tile, columns), lambda i: (i, 0))

    def whole(shape, mode=None):
        return pl.BlockSpec(shape, lambda i: (0, 0), pipeline_mode=mode)

    once = pl.Buffered(1)

    def square(index):
        return pl.BlockSpec((width, width), lambda i: (0, index), pipeline_mode=once)

    narrow = jax.ShapeDtypeStruct((tokens, width), bf16)
    wide = jax.ShapeDtypeStruct((tokens, hidden_units), bf16)
    return pl.pallas_call(
        middle_body,
        grid=(tokens // tile,),
        in_specs=[
            rows(width),
            rows(width),
            square(0),
            whole(vectors.shape, once),
            whole(bias_up.shape, once),
        ]
        + [square(1 + c) for c in range(2 * blocks)]
        + [rows(width // GROUPS)] * GROUPS,
        out_specs=[rows(width // GROUPS)] * GROUPS
        + [
            rows(width),
            rows(width),
            rows(width),
            rows(hidden_units),
            rows(hidden_units),
            rows(width),
            whole((8, width)),
            whole((1, hidden_units)),
        ],
        out_shape=[jax.ShapeDtypeStruct((tokens, width // GROUPS), bf16)] * GROUPS
        + [
            narrow,
            narrow,
            narrow,
            wide,
            wide,
            narrow,
            jax.ShapeDtypeStruct((8, width), f32),
            jax.ShapeDtypeStruct((1, hidden_units), f32),
        ],
        scratch_shapes=[pltpu.VMEM((tile, hidden_units), f32)],
        cost_estimate=pl.CostEstimate(
            flops=6 * tokens * width * (2 * hidden_units + width), transcendentals=0, bytes_accessed=0
        ),
        name="middle",
    )(
        x, g, w_packed, vectors, bias_up, *[w_packed] * (2 * blocks), *contexts
    )


def send(part, axis, size, target):
    return lax.ppermute(part, axis, [(i, target(i)) for i in range(size)])


def blocks_first(array, shards, blocks):
    split = array.reshape(array.shape[0], shards, blocks, -1)
    return split.transpose(0, 2, 1, 3).reshape(array.shape)


def shards_first(array, shards, blocks):
    return blocks_first(array, blocks, shards)


def gather_rows(part):
    return lax.all_gather(part, "shard", axis=0, tiled=True)


def reduce_rows(grad):
    return lax.psum_scatter(grad, "shard", scatter_dimension=0, tiled=True)


def reduce_parts(piece, parts):
    total = piece.astype(f32)
    for shift in range(1, parts):
        total = total + send(piece, "seq", parts, lambda i: (i + shift) % parts).astype(f32)
    return total


def after(value, *earlier):
    return lax.optimization_barrier((value,) + earlier)


def to_whole(rows, parts):
    count = rows.shape[0] * rows.shape[1] // parts
    blocks = rows.reshape((parts, count) + rows.shape[2:])
    index = lax.axis_index("seq")
    whole = jnp.zeros((count, parts) + rows.shape[2:], rows.dtype)
    for shift in range(parts):
        block = lax.dynamic_index_in_dim(blocks, (index + shift) % parts, 0, keepdims=False)
        if shift:
            block = lax.ppermute(block, "seq", [(i, (i + shift) % parts) for i in range(parts)])
        whole = lax.dynamic_update_index_in_dim(whole, block, (index - shift) % parts, 1)
    return whole.reshape((count, parts * rows.shape[2]) + rows.shape[3:])


def to_parts(rows, parts, shape):
    count = rows.shape[0]
    blocks = rows.reshape((count, parts, rows.shape[1] // parts) + rows.shape[2:])
    index = lax.axis_index("seq")
    back = jnp.zeros((parts, count) + blocks.shape[2:], rows.dtype)
    for shift in range(parts):
        block = lax.dynamic_index_in_dim(blocks, (index + shift) % parts, 1, keepdims=False)
        if shift:
            block = lax.ppermute(block, "seq", [(i, (i + shift) % parts) for i in range(parts)])
        back = lax.dynamic_update_index_in_dim(back, block, (index - shift) % parts, 0)
    return back.reshape(shape)


def local(
    shards, parts, hidden, cotangent, segments, w_qkv, bias_q, bias_v, w_out, bias_out, norm1_gain,
    norm1_bias, w_up, bias_up, w_down, bias_down, norm2_gain, norm2_bias,
):
    width = hidden.shape[3]
    owned_rows = w_qkv.shape[0]
    columns = w_qkv.shape[1]
    narrow = jnp.concatenate(
        [bias_q, bias_v, bias_out, norm1_gain, norm1_bias, bias_down, norm2_gain, norm2_bias]
    )
    small = jnp.concatenate([narrow, bias_up]).reshape(owned_rows, -1)
    spare = -small.shape[1] % UNIT
    packed = jnp.concatenate([w_qkv, jnp.pad(small, ((0, 0), (0, spare)))], axis=1)
    doc = to_whole(segments, parts)
    x = to_whole(hidden, parts)
    packed_full = gather_rows(packed)
    full_qkv = packed_full[:, :columns]
    small_full = packed_full[:, columns : columns + small.shape[1]].reshape(shards, -1).astype(f32)
    split = narrow.shape[0]
    vectors = small_full[:, :split].reshape(shards, 8, -1).transpose(1, 0, 2).reshape(8, width)
    full_bias_up = blocks_first(small_full[:, split:].reshape(1, -1), shards, w_down.shape[0] // owned_rows)
    blocks = w_down.shape[0] // owned_rows
    rest = jnp.concatenate(
        [w_out, blocks_first(w_up, shards, blocks)]
        + [w_down[b * owned_rows : (b + 1) * owned_rows] for b in range(blocks)],
        axis=1,
    )
    rest, packed_full = after(rest, packed_full)
    rest_full = gather_rows(rest)
    ahead = width + w_up.shape[1]

    count, seq_length = doc.shape
    tokens = count * seq_length
    start, size = key_windows(doc)
    doc_col = doc[:, :, None]
    doc_row = doc[:, None, :]
    x_rows = x.reshape(tokens, width)
    g = to_whole(cotangent, parts)
    offsets = jnp.concatenate([vectors[0], jnp.zeros_like(vectors[0]), vectors[1]])
    proj = (dot(x_rows, full_qkv) + offsets).astype(bf16).reshape(count, seq_length, -1)
    context, lse = attend_forward(proj, start, size, doc_col, doc_row, 0)
    context_rows = context.reshape(tokens, width)
    results = middle(
        x_rows,
        [context_rows],
        g.reshape(tokens, width),
        rest_full,
        vectors[2:],
        full_bias_up,
    )
    d_context, out, d_attn, h1, act, d_up, d_down, sums, sums_up = results
    grad_rest = jnp.concatenate(
        [
            dot(context_rows, d_attn, TN).astype(bf16),
            dot(h1, d_up, TN).astype(bf16),
        ]
        + [
            dot(act[:, b * width : (b + 1) * width], d_down, TN).astype(bf16)
            for b in range(blocks)
        ],
        axis=1,
    )
    d_context, out, grad_rest = after(d_context, out, grad_rest)
    layer_out = to_parts(out.reshape(count, seq_length, width), parts, hidden.shape)
    grad_rest = reduce_rows(grad_rest)
    d_proj, d_sums = attend_backward(
        proj,
        start,
        size,
        doc_col,
        doc_row,
        context,
        d_context.reshape(count, seq_length, width),
        lse,
        0,
    )
    d_rows = [d_proj[index].reshape(tokens, width) for index in range(3)]
    stacked = jnp.concatenate([jnp.sum(d_sums, axis=0), sums[:6]], axis=0)
    stacked = stacked.reshape(8, shards, -1).transpose(1, 0, 2).reshape(shards, -1)
    sums_up = shards_first(sums_up, shards, blocks)
    stacked = jnp.concatenate([stacked, sums_up.reshape(shards, -1)], axis=1)
    stacked = jnp.pad(stacked.reshape(width, -1), ((0, 0), (0, spare))).astype(bf16)
    grad_packed = jnp.concatenate(
        [dot(x_rows, d, TN).astype(bf16) for d in d_rows] + [stacked], axis=1
    )
    d_attn, grad_packed = after(d_attn, grad_packed)
    grad_packed = reduce_rows(grad_packed)
    grad_x = d_attn.astype(f32)
    for index, d in enumerate(d_rows):
        grad_x = grad_x + dot(d, full_qkv[:, index * width : (index + 1) * width], NT)
    grad_x = grad_x.astype(bf16).reshape(count, seq_length, width)
    grad_hidden = to_parts(grad_x, parts, hidden.shape)
    grad_rest = reduce_parts(grad_rest, parts)
    grad_out = grad_rest[:, :width]
    grad_up = shards_first(grad_rest[:, width:ahead], shards, blocks)
    grad_down = jnp.concatenate(
        [grad_rest[:, ahead + b * width : ahead + (b + 1) * width] for b in range(blocks)]
    )
    grad_packed = reduce_parts(grad_packed, parts)
    totals = grad_packed[:, columns : columns + small.shape[1]].reshape(-1)
    owned = totals[:split].reshape(8, -1)
    return (
        layer_out,
        grad_hidden,
        grad_packed[:, :columns],
        owned[0],
        owned[1],
        grad_out,
        owned[2],
        owned[3],
        owned[4],
        grad_up,
        totals[split:],
        grad_down,
        owned[5],
        owned[6],
        owned[7],
    )


def whole_step(shards, parts, *arguments):
    return local(shards, parts, *arguments)


def solution(mesh):
    tokens = P(None, "shard", "seq", None)
    matrix = P("shard", None)
    vector = P("shard")
    params = (
        matrix, vector, vector, matrix, vector, vector, vector, matrix, vector, matrix, vector,
        vector, vector,
    )
    return jax.shard_map(
        functools.partial(whole_step, mesh.shape["shard"], mesh.shape["seq"]),
        mesh=mesh,
        in_specs=(tokens, tokens, P(None, "shard", "seq")) + params,
        out_specs=(tokens, tokens) + params,
        check_vma=False,
    )
```

```python
import functools

import jax
import jax.numpy as jnp
from jax import lax
from jax.experimental import pallas as pl
from jax.experimental.pallas import tpu as pltpu
from jax.sharding import PartitionSpec as P


HD = 64
PAIR = 2 * HD
QB = 256
UNIT = 128
GROUPS = 1
eps_norm = 1e-05
masked_score = -1e30
bf16 = jnp.bfloat16
f32 = jnp.float32
NT = (((1,), (1,)), ((), ()))
TN = (((0,), (0,)), ((), ()))


def dot(a, b, dims=(((1,), (0,)), ((), ()))):
    return lax.dot_general(a, b, dims, preferred_element_type=f32)


def window_sizes(seq_length):
    units = seq_length // UNIT
    sizes = [n for n in (2, 3, 4, 5, 6) if n < units]
    return sizes + [units]


def key_windows(doc):
    _, seq_length = doc.shape
    first_doc = doc[:, ::QB]
    last_doc = doc[:, QB - 1 :: QB]
    low = jnp.sum((doc[:, None, :] < first_doc[:, :, None]).astype(jnp.int32), axis=2)
    high = jnp.sum((doc[:, None, :] <= last_doc[:, :, None]).astype(jnp.int32), axis=2)
    low_unit = low // UNIT
    need = (high + UNIT - 1) // UNIT - low_unit
    sizes = window_sizes(seq_length)
    size = jnp.full_like(need, sizes[-1])
    for n in sizes[::-1]:
        size = jnp.where(need <= n, n, size)
    start = jnp.minimum(low_unit, seq_length // UNIT - size)
    return start, size


def head_masks():
    lane = lax.broadcasted_iota(jnp.int32, (1, PAIR), 1)
    first = (lane < HD).astype(f32)
    return first.astype(bf16), (1.0 - first).astype(bf16)


def fwd_body(start_ref, size_ref, q_ref, k_ref, v_ref, dcol_ref, drow_ref, o_ref, lse_ref):
    item = pl.program_id(0)
    seq_length = q_ref.shape[0]
    masks = head_masks()
    first_lane = lax.broadcasted_iota(jnp.int32, (QB, PAIR), 1) < HD

    def step(i, carry):
        rows = pl.ds(pl.multiple_of(i * QB, QB), QB)
        for n in window_sizes(seq_length):

            @pl.when(size_ref[item, i] == n)
            def _():
                keys = pl.ds(pl.multiple_of(start_ref[item, i] * UNIT, UNIT), n * UNIT)
                q = q_ref[rows, :] * jnp.asarray(HD**-0.5, bf16)
                k = k_ref[keys, :]
                v = v_ref[keys, :]
                same = dcol_ref[rows, :] == drow_ref[:, keys]
                outs = []
                lses = []
                for h in range(2):
                    s = jnp.where(same, dot(q * masks[h], k, NT), masked_score)
                    top = jnp.max(s, axis=1, keepdims=True)
                    p = jnp.exp(s - top)
                    total = jnp.sum(p, axis=1, keepdims=True)
                    outs.append(dot(p.astype(bf16), v) * (1.0 / total))
                    lses.append(top + jnp.log(total))
                o_ref[rows, :] = jnp.where(first_lane, outs[0], outs[1]).astype(bf16)
                lse = jnp.where(first_lane, lses[0], lses[1]).T
                lse_ref[0:1, rows] = lse[0:1, :]
                lse_ref[1:2, rows] = lse[HD : HD + 1, :]

        return carry

    lax.fori_loop(0, seq_length // QB, step, 0)


def column_block(seq_length, base):
    return pl.BlockSpec((None, seq_length, PAIR), lambda s, p, *_: (s, 0, p + base))


def attend_forward(proj, start, size, doc_col, doc_row, group):
    count, seq_length, columns = proj.shape
    all_pairs = columns // 3 // PAIR
    pairs = all_pairs // GROUPS

    def part(index):
        return column_block(seq_length, index * all_pairs + group * pairs)

    return pl.pallas_call(
        fwd_body,
        grid_spec=pltpu.PrefetchScalarGridSpec(
            num_scalar_prefetch=2,
            grid=(count, pairs),
            in_specs=[
                part(0),
                part(1),
                part(2),
                pl.BlockSpec((None, seq_length, 1), lambda s, p, *_: (s, 0, 0)),
                pl.BlockSpec((None, 1, seq_length), lambda s, p, *_: (s, 0, 0)),
            ],
            out_specs=[
                column_block(seq_length, 0),
                pl.BlockSpec((None, None, 2, seq_length), lambda s, p, *_: (s, p, 0, 0)),
            ],
        ),
        out_shape=[
            jax.ShapeDtypeStruct((count, seq_length, pairs * PAIR), bf16),
            jax.ShapeDtypeStruct((count, pairs, 2, seq_length), f32),
        ],
        cost_estimate=pl.CostEstimate(
            flops=16 * count * pairs * seq_length**2 * PAIR, transcendentals=0, bytes_accessed=0
        ),
        name="attend_forward",
    )(start, size, proj, proj, proj, doc_col, doc_row)


def bwd_body(
    start_ref, size_ref, q_ref, k_ref, v_ref, dcol_ref, drow_ref, o_ref, do_ref, lse_ref,
    grad_ref, sums_ref, dk_acc, dv_acc,
):
    item = pl.program_id(0)
    seq_length = q_ref.shape[0]
    masks = head_masks()
    first_lane = lax.broadcasted_iota(jnp.int32, (QB, PAIR), 1) < HD
    dk_acc[...] = jnp.zeros_like(dk_acc)
    dv_acc[...] = jnp.zeros_like(dv_acc)
    sums_ref[...] = jnp.zeros_like(sums_ref)

    def step(i, carry):
        rows = pl.ds(pl.multiple_of(i * QB, QB), QB)
        for n in window_sizes(seq_length):

            @pl.when(size_ref[item, i] == n)
            def _():
                keys = pl.ds(pl.multiple_of(start_ref[item, i] * UNIT, UNIT), n * UNIT)
                q = q_ref[rows, :] * jnp.asarray(HD**-0.5, bf16)
                k = k_ref[keys, :]
                v = v_ref[keys, :]
                do = do_ref[rows, :]
                same = dcol_ref[keys, :] == drow_ref[:, rows]
                products = (do.astype(f32) * o_ref[rows, :].astype(f32)).T
                dqs = []
                dk = dv = None
                for h in range(2):
                    qh = q * masks[h]
                    doh = do * masks[h]
                    inner = jnp.sum(products[h * HD : (h + 1) * HD, :], axis=0, keepdims=True)
                    s = dot(k, qh, NT) - lse_ref[h : h + 1, rows]
                    p = jnp.exp(jnp.where(same, s, masked_score))
                    ds = (p * (dot(v, doh, NT) - inner)).astype(bf16)
                    dv_part = dot(p.astype(bf16), doh)
                    dk_part = dot(ds, qh)
                    dv = dv_part if dv is None else dv + dv_part
                    dk = dk_part if dk is None else dk + dk_part
                    dqs.append(dot(ds, k, TN))
                dk_acc[keys, :] += dk
                dv_acc[keys, :] += dv
                dq = (jnp.where(first_lane, dqs[0], dqs[1]) * (HD**-0.5)).astype(bf16)
                grad_ref[0, rows, :] = dq
                sums_ref[0:1, :] += jnp.sum(dq.astype(f32), axis=0, keepdims=True)

        return carry

    lax.fori_loop(0, seq_length // QB, step, 0)
    grad_ref[1] = dk_acc[...].astype(bf16)
    dv = dv_acc[...].astype(bf16)
    grad_ref[2] = dv
    sums_ref[1:2, :] = jnp.sum(dv.astype(f32), axis=0, keepdims=True)


def attend_backward(proj, start, size, doc_col, doc_row, context, d_context, lse, group):
    count, seq_length, columns = proj.shape
    all_pairs = columns // 3 // PAIR
    pairs = all_pairs // GROUPS

    def part(index):
        return column_block(seq_length, index * all_pairs + group * pairs)

    return pl.pallas_call(
        bwd_body,
        grid_spec=pltpu.PrefetchScalarGridSpec(
            num_scalar_prefetch=2,
            grid=(count, pairs),
            in_specs=[
                part(0),
                part(1),
                part(2),
                pl.BlockSpec((None, seq_length, 1), lambda s, p, *_: (s, 0, 0)),
                pl.BlockSpec((None, 1, seq_length), lambda s, p, *_: (s, 0, 0)),
                column_block(seq_length, 0),
                column_block(seq_length, 0),
                pl.BlockSpec((None, None, 2, seq_length), lambda s, p, *_: (s, p, 0, 0)),
            ],
            out_specs=[
                pl.BlockSpec((3, None, seq_length, PAIR), lambda s, p, *_: (0, s, 0, p)),
                pl.BlockSpec((None, 2, PAIR), lambda s, p, *_: (s, 0, p)),
            ],
            scratch_shapes=[
                pltpu.VMEM((seq_length, PAIR), f32),
                pltpu.VMEM((seq_length, PAIR), f32),
            ],
        ),
        out_shape=[
            jax.ShapeDtypeStruct((3, count, seq_length, pairs * PAIR), bf16),
            jax.ShapeDtypeStruct((count, 2, pairs * PAIR), f32),
        ],
        cost_estimate=pl.CostEstimate(
            flops=24 * count * pairs * seq_length**2 * PAIR, transcendentals=0, bytes_accessed=0
        ),
        name="attend_backward",
    )(start, size, proj, proj, proj, doc_col, doc_row, context, d_context, lse)


def norm_parts(resid):
    center = jnp.mean(resid, axis=1, keepdims=True)
    deviate = resid - center
    spread = jnp.mean(deviate * deviate, axis=1, keepdims=True)
    rstd = lax.rsqrt(spread + eps_norm)
    return deviate * rstd, rstd


def norm_back(grad, xhat, rstd):
    return rstd * (
        grad
        - jnp.mean(grad, axis=1, keepdims=True)
        - xhat * jnp.mean(grad * xhat, axis=1, keepdims=True)
    )


def middle_body(
    x_ref, g_ref, w_out_ref, vec_ref, bias_up_ref, *refs
):
    chunk = x_ref.shape[1]
    chunks = [slice(c, c + chunk) for c in range(0, bias_up_ref.shape[1], chunk)]
    w_up_refs, refs = refs[: len(chunks)], refs[len(chunks) :]
    w_down_refs, refs = refs[: len(chunks)], refs[len(chunks) :]
    o_refs, refs = refs[:GROUPS], refs[GROUPS:]
    d_context_refs, refs = refs[:GROUPS], refs[GROUPS:]
    out_ref, d_attn_ref, h1_ref, act_ref, d_up_ref, d_down_ref, sums_ref, sums_up_ref, slope_ref = refs
    span = o_refs[0].shape[1]

    @pl.when(pl.program_id(0) == 0)
    def _():
        sums_ref[...] = jnp.zeros_like(sums_ref)
        sums_up_ref[...] = jnp.zeros_like(sums_up_ref)

    bias_out, gain1, shift1, bias_down, gain2, shift2 = (vec_ref[r : r + 1, :] for r in range(6))
    resid1 = x_ref[...].astype(f32) + bias_out
    for j, o_ref in enumerate(o_refs):
        resid1 = resid1 + dot(o_ref[...], w_out_ref[j * span : (j + 1) * span, :])
    xhat1, rstd1 = norm_parts(resid1)
    h1 = xhat1 * gain1 + shift1
    h1_low = h1.astype(bf16)
    h1_ref[...] = h1_low
    resid2 = h1 + bias_down
    for c, w_up_ref, w_down_ref in zip(chunks, w_up_refs, w_down_refs):
        up = dot(h1_low, w_up_ref[...]) + bias_up_ref[:, c]
        cdf = 0.5 + 0.5 * lax.erf(up * (0.5**0.5))
        act = (up * cdf).astype(bf16)
        slope_ref[:, c] = cdf + up * jnp.exp(-0.5 * up * up) * 0.3989422804014327
        act_ref[:, c] = act
        resid2 = resid2 + dot(act, w_down_ref[...])
    xhat2, rstd2 = norm_parts(resid2)
    out_ref[...] = (xhat2 * gain2 + shift2).astype(bf16)
    g = g_ref[...].astype(f32)
    d_resid2 = norm_back(g * gain2, xhat2, rstd2)
    d_down = d_resid2.astype(bf16)
    d_down_ref[...] = d_down
    d_h1 = d_resid2
    for c, w_up_ref, w_down_ref in zip(chunks, w_up_refs, w_down_refs):
        d_up = (dot(d_down, w_down_ref[...], NT) * slope_ref[:, c]).astype(bf16)
        d_up_ref[:, c] = d_up
        sums_up_ref[:, c] += jnp.sum(d_up.astype(f32), axis=0, keepdims=True)
        d_h1 = d_h1 + dot(d_up, w_up_ref[...], NT)
    d_attn = norm_back(d_h1 * gain1, xhat1, rstd1).astype(bf16)
    d_attn_ref[...] = d_attn
    for j, ref in enumerate(d_context_refs):
        ref[...] = dot(d_attn, w_out_ref[j * span : (j + 1) * span, :], NT).astype(bf16)
    rows = (d_attn.astype(f32), d_h1 * xhat1, d_h1, d_down.astype(f32), g * xhat2, g)
    for r, value in enumerate(rows):
        sums_ref[r : r + 1, :] += jnp.sum(value, axis=0, keepdims=True)


def middle(x, contexts, g, w_packed, vectors, bias_up):
    tokens, width = x.shape
    hidden_units = bias_up.shape[1]
    blocks = hidden_units // width
    tile = QB

    def rows(columns):
        return pl.BlockSpec((tile, columns), lambda i: (i, 0))

    def whole(shape, mode=None):
        return pl.BlockSpec(shape, lambda i: (0, 0), pipeline_mode=mode)

    once = pl.Buffered(1)

    def square(index):
        return pl.BlockSpec((width, width), lambda i: (0, index), pipeline_mode=once)

    narrow = jax.ShapeDtypeStruct((tokens, width), bf16)
    wide = jax.ShapeDtypeStruct((tokens, hidden_units), bf16)
    return pl.pallas_call(
        middle_body,
        grid=(tokens // tile,),
        in_specs=[
            rows(width),
            rows(width),
            square(0),
            whole(vectors.shape, once),
            whole(bias_up.shape, once),
        ]
        + [square(1 + c) for c in range(2 * blocks)]
        + [rows(width // GROUPS)] * GROUPS,
        out_specs=[rows(width // GROUPS)] * GROUPS
        + [
            rows(width),
            rows(width),
            rows(width),
            rows(hidden_units),
            rows(hidden_units),
            rows(width),
            whole((8, width)),
            whole((1, hidden_units)),
        ],
        out_shape=[jax.ShapeDtypeStruct((tokens, width // GROUPS), bf16)] * GROUPS
        + [
            narrow,
            narrow,
            narrow,
            wide,
            wide,
            narrow,
            jax.ShapeDtypeStruct((8, width), f32),
            jax.ShapeDtypeStruct((1, hidden_units), f32),
        ],
        scratch_shapes=[pltpu.VMEM((tile, hidden_units), f32)],
        cost_estimate=pl.CostEstimate(
            flops=6 * tokens * width * (2 * hidden_units + width), transcendentals=0, bytes_accessed=0
        ),
        name="middle",
    )(
        x, g, w_packed, vectors, bias_up, *[w_packed] * (2 * blocks), *contexts
    )


def send(part, axis, size, target):
    return lax.ppermute(part, axis, [(i, target(i)) for i in range(size)])


def blocks_first(array, shards, blocks):
    split = array.reshape(array.shape[0], shards, blocks, -1)
    return split.transpose(0, 2, 1, 3).reshape(array.shape)


def shards_first(array, shards, blocks):
    return blocks_first(array, blocks, shards)


def gather_rows(part):
    return lax.all_gather(part, "shard", axis=0, tiled=True)


def reduce_rows(grad):
    return lax.psum_scatter(grad, "shard", scatter_dimension=0, tiled=True)


def reduce_parts(piece, parts):
    total = piece.astype(f32)
    for shift in range(1, parts):
        total = total + send(piece, "seq", parts, lambda i: (i + shift) % parts).astype(f32)
    return total


def after(value, *earlier):
    return lax.optimization_barrier((value,) + earlier)


def to_whole(rows, parts):
    count = rows.shape[0] * rows.shape[1] // parts
    blocks = rows.reshape((parts, count) + rows.shape[2:])
    index = lax.axis_index("seq")
    whole = jnp.zeros((count, parts) + rows.shape[2:], rows.dtype)
    for shift in range(parts):
        block = lax.dynamic_index_in_dim(blocks, (index + shift) % parts, 0, keepdims=False)
        if shift:
            block = lax.ppermute(block, "seq", [(i, (i + shift) % parts) for i in range(parts)])
        whole = lax.dynamic_update_index_in_dim(whole, block, (index - shift) % parts, 1)
    return whole.reshape((count, parts * rows.shape[2]) + rows.shape[3:])


def to_parts(rows, parts, shape):
    count = rows.shape[0]
    blocks = rows.reshape((count, parts, rows.shape[1] // parts) + rows.shape[2:])
    index = lax.axis_index("seq")
    back = jnp.zeros((parts, count) + blocks.shape[2:], rows.dtype)
    for shift in range(parts):
        block = lax.dynamic_index_in_dim(blocks, (index + shift) % parts, 1, keepdims=False)
        if shift:
            block = lax.ppermute(block, "seq", [(i, (i + shift) % parts) for i in range(parts)])
        back = lax.dynamic_update_index_in_dim(back, block, (index - shift) % parts, 0)
    return back.reshape(shape)


def local(
    shards, parts, hidden, cotangent, segments, w_qkv, bias_q, bias_v, w_out, bias_out, norm1_gain,
    norm1_bias, w_up, bias_up, w_down, bias_down, norm2_gain, norm2_bias,
):
    width = hidden.shape[3]
    owned_rows = w_qkv.shape[0]
    columns = w_qkv.shape[1]
    blocks = w_down.shape[0] // owned_rows
    narrow = [
        bias_q, bias_v, bias_out, norm1_gain, norm1_bias, bias_down, norm2_gain, norm2_bias,
    ]
    small = jnp.stack(narrow + [row for row in bias_up.reshape(blocks, -1)], axis=1)
    spare = -small.shape[1] % UNIT
    packed = jnp.concatenate([w_qkv, jnp.pad(small, ((0, 0), (0, spare)))], axis=1)
    x = to_whole(hidden, parts)
    doc = to_whole(segments, parts)
    start, size = key_windows(doc)
    doc_col = doc[:, :, None]
    doc_row = doc[:, None, :]
    packed_full = gather_rows(packed)
    full_qkv = packed_full[:, :columns]
    vectors = packed_full[:, columns:].astype(f32).T
    full_bias_up = vectors[8 : 8 + blocks].reshape(1, -1)
    rest = jnp.concatenate(
        [w_out, blocks_first(w_up, shards, blocks)]
        + [w_down[b * owned_rows : (b + 1) * owned_rows] for b in range(blocks)],
        axis=1,
    )
    rest, packed_full = after(rest, packed_full)
    rest_full = gather_rows(rest)

    count, seq_length = doc.shape
    tokens = count * seq_length
    x_rows = x.reshape(tokens, width)
    g = to_whole(cotangent, parts)
    offsets = jnp.concatenate([vectors[0], jnp.zeros_like(vectors[0]), vectors[1]])
    proj = (dot(x_rows, full_qkv) + offsets).astype(bf16).reshape(count, seq_length, -1)
    context, lse = attend_forward(proj, start, size, doc_col, doc_row, 0)
    context_rows = context.reshape(tokens, width)
    results = middle(
        x_rows,
        [context_rows],
        g.reshape(tokens, width),
        rest_full,
        vectors[2:8],
        full_bias_up,
    )
    d_context, out, d_attn, h1, act, d_up, d_down, sums, sums_up = results

    def grad_block(rows, block):
        return dot(rows[:, block * width : (block + 1) * width], d_down, TN).astype(bf16)

    later = blocks // 2
    grad_first = jnp.concatenate(
        [dot(h1, d_up, TN).astype(bf16)] + [grad_block(act, b) for b in range(later, blocks)],
        axis=1,
    )
    d_context, out, act, context_rows, grad_first = after(
        d_context, out, act, context_rows, grad_first
    )
    layer_out = to_parts(out.reshape(count, seq_length, width), parts, hidden.shape)
    grad_first = reduce_rows(grad_first)
    d_proj, d_sums = attend_backward(
        proj,
        start,
        size,
        doc_col,
        doc_row,
        context,
        d_context.reshape(count, seq_length, width),
        lse,
        0,
    )
    d_rows = [d_proj[index].reshape(tokens, width) for index in range(3)]
    stacked = [jnp.sum(d_sums, axis=0), sums[:6], sums_up.reshape(blocks, -1)]
    stacked = jnp.concatenate(stacked).T.astype(bf16)
    grad_packed = jnp.concatenate(
        [dot(x_rows, d, TN).astype(bf16) for d in d_rows]
        + [dot(context_rows, d_attn, TN).astype(bf16)]
        + [grad_block(act, b) for b in range(later)]
        + [jnp.pad(stacked, ((0, 0), (0, spare)))],
        axis=1,
    )
    d_attn, grad_packed = after(d_attn, grad_packed)
    grad_packed = reduce_rows(grad_packed)
    grad_x = d_attn.astype(f32)
    for index, d in enumerate(d_rows):
        grad_x = grad_x + dot(d, full_qkv[:, index * width : (index + 1) * width], NT)
    grad_x = grad_x.astype(bf16).reshape(count, seq_length, width)
    grad_hidden = to_parts(grad_x, parts, hidden.shape)
    grad_first = reduce_parts(grad_first, parts)
    grad_up = shards_first(grad_first[:, : w_up.shape[1]], shards, blocks)
    grad_packed = reduce_parts(grad_packed, parts)

    def owned_block(rows, index):
        return rows[:, index * width : (index + 1) * width]

    grad_out = owned_block(grad_packed, 3)
    grad_down = jnp.concatenate(
        [owned_block(grad_packed, 4 + b) for b in range(later)]
        + [owned_block(grad_first, b) for b in range(blocks, 2 * blocks - later)]
    )
    totals = grad_packed[:, (4 + later) * width :].T
    owned = totals[:8]
    grad_bias_up = totals[8 : 8 + blocks].reshape(-1)
    return (
        layer_out,
        grad_hidden,
        grad_packed[:, :columns],
        owned[0],
        owned[1],
        grad_out,
        owned[2],
        owned[3],
        owned[4],
        grad_up,
        grad_bias_up,
        grad_down,
        owned[5],
        owned[6],
        owned[7],
    )


def whole_step(shards, parts, *arguments):
    return local(shards, parts, *arguments)


def solution(mesh):
    tokens = P(None, "shard", "seq", None)
    matrix = P("shard", None)
    vector = P("shard")
    params = (
        matrix, vector, vector, matrix, vector, vector, vector, matrix, vector, matrix, vector,
        vector, vector,
    )
    return jax.shard_map(
        functools.partial(whole_step, mesh.shape["shard"], mesh.shape["seq"]),
        mesh=mesh,
        in_specs=(tokens, tokens, P(None, "shard", "seq")) + params,
        out_specs=(tokens, tokens) + params,
        check_vma=False,
    )
```
